32 devices in a mesh: row: 8 (over y, x, core), col: 4 (over z).
Axes of the slice: x: 2, y: 2, z: 4, core: 2. Of those that a mesh axis runs over, the one named last changes fastest.
Arguments:
- source_features: bfloat16 [4, 2048, 256], P('col', 'row'), may hold values from -500 to 500
- target_features: bfloat16 [8192, 256], P(('row', 'col')), may hold values from -6 to 6
- weight: bfloat16 [256, 256], replicated, may hold values from -0.375 to 0.375
- score_source: float32 [4, 64], replicated, may hold values from -0.75 to 0.75
- score_target: float32 [4, 64], replicated, may hold values from -0.75 to 0.75
- out_bias: float32 [256], replicated, may hold values from -3 to 3
- block_list: int32 [8, 4, 48], P('row', 'col'), may hold values from 0 to 127, as said below
- block_count: int32 [8, 4], P('row', 'col'), may hold values from 8 to 48, as said below
- edge_bits: int32 [8, 4, 48, 16, 128], P('row', 'col'), may hold values from 0 to 255, as said below
Outputs:
- updated: bfloat16 [8192, 256], P(('row', 'col'))
The draws below stay inside these ranges and needn't reach their ends.
Inputs may be any that keep to these rules, and one draw needn't show every extreme that they name: `block_list`: slot s of tile (r, c) names target block p // 16 and source block p % 16 of the tile; the first block_count[r, c] slots of a tile name distinct blocks and later slots are unused. `block_count`: some tile holds 48 blocks. `edge_bits`: bit b of entry [r, c, s, w, i] marks the edge from source 8 w + b to target i of the block in slot s. Some targets have no edge.
All inputs are finite; a program needn't handle non-finite values.
Results may differ from the reference program's by a relative error of at most 0.007.
The reference program's roundings to bfloat16 on the way (of `projected` and `weights`) count: a program that leaves them out, or rounds other values in their place, can miss the bound.
Values may be sent and summed in bfloat16 or wider, within the bound.
No kernel may reach another device: no remote copies, remote signals or barrier semaphores. Data moves between devices by JAX's collectives and lax.ppermute only.
A program may use at most 64 MiB of HBM per device.

```python
import jax
import jax.numpy as jnp
from jax import lax

D = 256
H = 4
HD = 64
BLK = 128
DB = 8
SB = 16
MAXB = 48
NSRC = 8192
NDST = 8192
N_ROW = 8
N_COL = 4


def graph_tables(key):
    base = jax.random.fold_in(key, 7)
    key_count, key_full, key_perm, key_bits, key_empty = jax.random.split(base, 5)
    tiles = N_ROW * N_COL
    lowest = max(1, MAXB // 6)
    counts = jax.random.randint(key_count, (tiles,), lowest, MAXB + 1).astype(jnp.int32)
    chosen = jax.random.randint(key_full, (), 0, tiles)
    counts = jnp.where(jnp.arange(tiles) == chosen, MAXB, counts).astype(jnp.int32)
    perm_keys = jax.random.split(key_perm, tiles)
    slots = jax.vmap(lambda one: jax.random.permutation(one, DB * SB)[:MAXB])(perm_keys).astype(jnp.int32)
    packed = jnp.zeros((tiles, MAXB, BLK // 8, BLK), jnp.int32)
    for bit in range(8):
        setting = jax.random.randint(jax.random.fold_in(key_bits, bit), (tiles, MAXB, BLK // 8, BLK), 0, 20) == 0
        packed = packed + jnp.where(setting, 1 << bit, 0).astype(jnp.int32)
    empty = jax.random.randint(key_empty, (N_ROW, DB * BLK), 0, 40) == 0
    tile_row = jnp.arange(tiles) // N_COL
    target = (slots // SB)[:, :, None] * BLK + jnp.arange(BLK)[None, None, :]
    blank = empty[tile_row[:, None, None], target]
    packed = jnp.where(blank[:, :, None, :], 0, packed).astype(jnp.int32)
    return (slots.reshape(N_ROW, N_COL, MAXB), counts.reshape(N_ROW, N_COL), packed.reshape(N_ROW, N_COL, MAXB, BLK // 8, BLK))


def draw_block_list(key, part):
    return graph_tables(key)[0]


def draw_block_count(key, part):
    return graph_tables(key)[1]


def draw_edge_bits(key, part):
    return graph_tables(key)[2]


def draw_source_features(key, part):
    key_base = jax.random.fold_in(jax.random.fold_in(key, 11), 0)
    shape = (N_COL, SB * BLK, D)
    values = jnp.clip(jax.random.normal(key_base, shape, jnp.float32), -8.0, 8.0)
    return values.astype(jnp.bfloat16)


def steps_of(key, dims, cuts, smallest, high):
    gain, own = 1.0, jax.random.fold_in(key, 6)
    for axis_at, shards_of in cuts:
        heights = jnp.exp(jax.random.uniform(jax.random.fold_in(own, axis_at), (shards_of,), jnp.float32, smallest / len(cuts), high / len(cuts)))
        gain = gain * jnp.repeat(heights, dims[axis_at] // shards_of).reshape([-1 if axis == axis_at else 1 for axis in range(len(dims))])
    return gain


def noise(own_key, shape, scale, reach, shards=(), kind=jnp.bfloat16):
    values = scale * jax.random.normal(own_key, shape, jnp.float32)
    if shards:
        values = values * steps_of(own_key, shape, shards, -0.22, 0.18)
    return jnp.clip(values, -reach, reach).astype(kind)


def setup_inputs(seed: int = 0) -> dict:
    seeds = jax.random.split(jax.random.key(seed), 10)
    return {
        "source_features": draw_source_features(jax.random.fold_in(seeds[9], 71), 0),
        "target_features": noise(seeds[1], (NDST, D), 1.0, 6.0, ((0, 32),)),
        "weight": noise(seeds[2], (D, H * HD), D ** -0.5, 0.375),
        "score_source": noise(seeds[3], (H, HD), HD ** -0.5, 0.75, (), jnp.float32),
        "score_target": noise(seeds[4], (H, HD), HD ** -0.5, 0.75, (), jnp.float32),
        "out_bias": noise(seeds[5], (H * HD,), 0.5, 3.0, (), jnp.float32),
        "block_list": draw_block_list(jax.random.fold_in(seeds[9], 71), 0),
        "block_count": draw_block_count(jax.random.fold_in(seeds[9], 71), 0),
        "edge_bits": draw_edge_bits(jax.random.fold_in(seeds[9], 71), 0),
    }


very_low = -1e30
slope = 0.2
per_step = 4


def unpack(packed):
    shifts = jnp.arange(8, dtype=jnp.int32)
    spread = jnp.right_shift(packed[:, None, :], shifts[None, :, None]) & 1
    return spread.reshape(packed.shape[0] * 8, packed.shape[1]) > 0


def block_scores(src_logits, dst_logits, position):
    dst_block = (position // SB).astype(jnp.int32)
    src_block = (position % SB).astype(jnp.int32)
    zero = jnp.zeros((), jnp.int32)
    head_count = src_logits.shape[0]
    from_src = lax.dynamic_slice(src_logits, (zero, src_block * BLK), (head_count, BLK))
    from_dst = lax.dynamic_slice(dst_logits, (zero, dst_block * BLK), (head_count, BLK))
    raw = from_src[:, :, None] + from_dst[:, None, :]
    return dst_block, src_block, jnp.where(raw > 0, raw, slope * raw)


def tile_max(src_logits, dst_logits, slots, live, packed, row_max):
    zero = jnp.zeros((), jnp.int32)
    head_count = src_logits.shape[0]

    def advance(group, row_max):
        first = jnp.asarray(group, jnp.int32) * per_step
        for member in range(per_step):
            slot = first + member
            edge_mask = unpack(packed[slot]) & (slot < live)
            dst_block, src_block, scores = block_scores(src_logits, dst_logits, slots[slot])
            block_max = jnp.max(jnp.where(edge_mask[None], scores, very_low), axis=1)
            prior = lax.dynamic_slice(row_max, (zero, dst_block * BLK), (head_count, BLK))
            row_max = lax.dynamic_update_slice(row_max, jnp.maximum(prior, block_max), (zero, dst_block * BLK))
        return row_max

    return lax.fori_loop(0, slots.shape[0] // per_step, advance, row_max)


def tile_sum(features, src_logits, dst_logits, slots, live, packed, row_max, carry):
    zero = jnp.zeros((), jnp.int32)
    head_count = src_logits.shape[0]
    out_width = features.shape[1]
    head_size = out_width // head_count

    def advance(group, carry):
        accum, denoms = carry
        first = jnp.asarray(group, jnp.int32) * per_step
        for member in range(per_step):
            slot = first + member
            edge_mask = unpack(packed[slot]) & (slot < live)
            dst_block, src_block, scores = block_scores(src_logits, dst_logits, slots[slot])
            prior_max = lax.dynamic_slice(row_max, (zero, dst_block * BLK), (head_count, BLK))
            numer = jnp.exp(jnp.where(edge_mask[None], scores - prior_max[:, None, :], very_low))
            old_denoms = lax.dynamic_slice(denoms, (dst_block * BLK, zero), (BLK, head_count))
            denoms = lax.dynamic_update_slice(denoms, old_denoms + jnp.sum(numer, axis=1).T, (dst_block * BLK, zero))
            weights = numer.astype(jnp.bfloat16)
            src_feats = lax.dynamic_slice(features, (src_block * BLK, zero), (BLK, out_width)).reshape(BLK, head_count, head_size)
            product = jnp.einsum("hji,jhk->ihk", weights.astype(jnp.float32), src_feats.astype(jnp.float32), precision=lax.Precision.HIGHEST).reshape(BLK, out_width)
            old_accum = lax.dynamic_slice(accum, (dst_block * BLK, zero), (BLK, out_width))
            accum = lax.dynamic_update_slice(accum, old_accum + product, (dst_block * BLK, zero))
        return accum, denoms

    return lax.fori_loop(0, slots.shape[0] // per_step, advance, carry)


def reference(source_features, target_features, weight, score_source, score_target, out_bias, block_list, block_count, edge_bits):
    head_count = H
    out_width = H * HD
    src_rows = SB * BLK
    dst_rows = DB * BLK
    zero = jnp.zeros((), jnp.int32)
    projected = jnp.dot(source_features.reshape(NSRC, D), weight, preferred_element_type=jnp.float32).astype(jnp.bfloat16)
    src_all = jnp.einsum("nhk,hk->hn", projected.reshape(NSRC, H, HD).astype(jnp.float32), score_source, precision=lax.Precision.HIGHEST)
    dst_proj = jnp.dot(target_features, weight, preferred_element_type=jnp.float32)
    dst_all = jnp.einsum("nhk,hk->hn", dst_proj.reshape(NDST, H, HD), score_target, precision=lax.Precision.HIGHEST)

    def row_block(index):
        index = index.astype(jnp.int32)
        dst_logits = lax.dynamic_slice(dst_all, (zero, index * dst_rows), (head_count, dst_rows))

        def column_max(column, row_max):
            column = jnp.asarray(column, jnp.int32)
            src_logits = lax.dynamic_slice(src_all, (zero, column * src_rows), (head_count, src_rows))
            return tile_max(src_logits, dst_logits, block_list[index, column], block_count[index, column], edge_bits[index, column], row_max)

        row_max = lax.fori_loop(0, N_COL, column_max, jnp.full((head_count, dst_rows), very_low, jnp.float32))

        def column_sum(column, carry):
            column = jnp.asarray(column, jnp.int32)
            src_logits = lax.dynamic_slice(src_all, (zero, column * src_rows), (head_count, src_rows))
            features = lax.dynamic_slice(projected, (column * src_rows, zero), (src_rows, out_width))
            return tile_sum(features, src_logits, dst_logits, block_list[index, column], block_count[index, column], edge_bits[index, column], row_max, carry)

        start = (jnp.zeros((dst_rows, out_width), jnp.float32), jnp.zeros((dst_rows, head_count), jnp.float32))
        accum, denoms = lax.fori_loop(0, N_COL, column_sum, start)
        blended = accum.reshape(dst_rows, head_count, HD) / jnp.maximum(denoms, 1.0)[:, :, None]
        return jax.nn.elu(blended.reshape(dst_rows, out_width) + out_bias).astype(jnp.bfloat16)

    stacked = lax.map(row_block, jnp.arange(N_ROW, dtype=jnp.int32))
    return stacked.reshape(NDST, out_width)
```

```python
import functools

import jax
import jax.numpy as jnp
from jax import lax
from jax.experimental import pallas as pl
from jax.experimental.pallas import tpu as pltpu
from jax.sharding import PartitionSpec as P

BLK = 128
GROUP = 4
very_low = -1e30
slope = 0.2
log2e = 1.4426950408889634
f32 = jnp.float32
bf16 = jnp.bfloat16
NT = (((1,), (1,)), ((), ()))


def leaky(z):
    return jnp.maximum(z, slope * z)


def block_rows(scores, width):
    heads, size = scores.shape
    tiled = jnp.concatenate([scores] * heads, axis=1)
    row = lax.broadcasted_iota(jnp.int32, tiled.shape, 0)
    column = lax.broadcasted_iota(jnp.int32, tiled.shape, 1)
    return jnp.where(column // size == row, tiled, 0.0)


def thirds(value):
    high = value.astype(bf16)
    rest = value - high.astype(f32)
    middle = rest.astype(bf16)
    low = (rest - middle.astype(f32)).astype(bf16)
    return high, middle, low


def target_kernel(x_ref, w_ref, score_ref, out_ref):
    rows = block_rows(score_ref[...], w_ref.shape[1])
    product = jnp.dot(x_ref[...], w_ref[...], preferred_element_type=f32)
    logits = lax.dot_general(
        rows, product, NT, precision=lax.Precision.HIGHEST, preferred_element_type=f32
    )
    out_ref[...] = logits * log2e


def tile_kernel(cfg, *refs):
    heads, size, src_blocks, dst_blocks, n_src, n_dst, row_axis, col_axis, split = cfg
    refs = list(refs)
    slots_ref, count_ref, bits_ref, w_ref, score_ref = refs[:5]
    x_refs = refs[5 : 5 + n_src]
    d_refs = refs[5 + n_src : 5 + n_src + n_dst]
    n_out = n_dst if split else 1
    out_refs = refs[5 + n_src + n_dst : 5 + n_src + n_dst + n_out]
    feats, spread, logit, top, total, accum = refs[5 + n_src + n_dst + n_out :]
    width = w_ref.shape[1]

    turned = w_ref[...].astype(f32).T.astype(bf16)
    parts = thirds(block_rows(score_ref[...], width))
    rows = jnp.concatenate([part.astype(f32) for part in parts], axis=0).astype(bf16)
    for k in range(n_src):
        x = x_refs[k][...]
        x = x.reshape(x.shape[-2], x.shape[-1])
        blocks = x.shape[0] // BLK
        first = (lax.axis_index(row_axis) ^ k) * blocks if n_src > 1 else 0
        projected = jnp.dot(x, w_ref[...], preferred_element_type=f32).astype(bf16)
        three = lax.dot_general(projected, rows, NT, preferred_element_type=f32)
        source = three[:, :heads] + three[:, heads : 2 * heads] + three[:, 2 * heads : 3 * heads]
        source = source * log2e
        across = lax.dot_general(turned, x, NT, preferred_element_type=f32).astype(bf16)
        for b in range(blocks):
            feats[first + b] = across[:, b * BLK : (b + 1) * BLK]
            for h in range(heads):
                column = source[b * BLK : (b + 1) * BLK, h : h + 1]
                spread[(first + b) * heads + h] = jnp.broadcast_to(column, (BLK, BLK))
    for k in range(n_dst):
        d = d_refs[k][...]
        blocks = d.shape[1] // BLK
        first = (lax.axis_index(col_axis) ^ k) * blocks if n_dst > 1 else 0
        for b in range(blocks):
            logit[first + b] = d[:, b * BLK : (b + 1) * BLK]
    top[...] = jnp.full(top.shape, very_low, f32)
    total[...] = jnp.zeros(total.shape, f32)
    accum[...] = jnp.zeros(accum.shape, f32)

    live = count_ref[0, 0]
    groups = (live + GROUP - 1) // GROUP
    bit = jnp.left_shift(1, lax.broadcasted_iota(jnp.int32, (1, 8, BLK), 1))

    def place(slot):
        p = slots_ref[0, 0, slot]
        return p // src_blocks, p % src_blocks

    def edges(slot):
        packed = jnp.where(slot < live, bits_ref[0, 0, slot], 0)
        return (packed[:, None, :] & bit) != 0

    def largest(group, carry):
        found = []
        for member in range(GROUP):
            slot = group * GROUP + member
            dst, src = place(slot)
            mask = edges(slot)
            for h in range(heads):
                s = spread[src * heads + h].reshape(BLK // 8, 8, BLK)
                found.append((dst, h, jnp.max(jnp.where(mask, s, very_low), axis=0)))
        for dst, h, value in found:
            top[dst * heads + h] = jnp.maximum(top[dst * heads + h], value)
        return carry

    lax.fori_loop(0, groups, largest, 0)

    for b in range(dst_blocks):
        best = [jnp.max(top[b * heads + h], axis=0, keepdims=True) for h in range(heads)]
        z = jnp.concatenate(best, axis=0) + logit[b]
        top[b * heads, :heads] = leaky(z)

    def gather(group, carry):
        sums = []
        for member in range(GROUP):
            slot = group * GROUP + member
            dst, src = place(slot)
            mask = edges(slot)
            feat = feats[src]
            products = []
            for h in range(heads):
                s = spread[src * heads + h].reshape(BLK // 8, 8, BLK)
                d = logit[dst, h : h + 1].reshape(1, 1, BLK)
                m = top[dst * heads, h : h + 1].reshape(1, 1, BLK)
                e = jnp.exp2(jnp.where(mask, leaky(s + d) - m, very_low))
                sums.append((dst, h, jnp.sum(e, axis=0)))
                weights = e.reshape(BLK, BLK).astype(bf16)
                products.append(
                    jnp.dot(
                        feat[h * size : (h + 1) * size],
                        weights,
                        preferred_element_type=f32,
                    )
                )
            sums.append((dst, -1, products))
        for dst, h, value in sums:
            if h >= 0:
                total[dst * heads + h] = total[dst * heads + h] + value
            else:
                for g in range(heads):
                    part = pl.ds(g * size, size)
                    accum[dst, part] = accum[dst, part] + value[g]
        return carry

    lax.fori_loop(0, groups, gather, 0)

    def write(out_ref, lanes, b):
        out_ref[:width, lanes] = accum[b].astype(bf16)
        m = top[b * heads, :heads]
        denom = [jnp.sum(total[b * heads + h], axis=0, keepdims=True) for h in range(heads)]
        stats = [part.astype(f32) for part in thirds(m)] + denom
        out_ref[width:, lanes] = jnp.concatenate(stats, axis=0).astype(bf16)

    if split:
        blocks = dst_blocks // n_dst
        for k in range(n_dst):
            first = (lax.axis_index(col_axis) ^ k) * blocks
            for b in range(blocks):
                write(out_refs[k], pl.ds(b * BLK, BLK), first + b)
    else:
        for b in range(dst_blocks):
            write(out_refs[0], pl.ds(b * BLK, BLK), b)


def merge_kernel(heads, *refs):
    *part_refs, bias_ref, out_ref = refs
    width = bias_ref.shape[1]
    size = width // heads
    stats = [ref[width:].astype(f32) for ref in part_refs]
    tops = [s[:heads] + s[heads : 2 * heads] + s[2 * heads : 3 * heads] for s in stats]
    best = functools.reduce(jnp.maximum, tops)
    scales = [jnp.exp2(t - best) for t in tops]
    denom = sum(scale * s[3 * heads :] for scale, s in zip(scales, stats))
    inverse = 1.0 / jnp.maximum(denom, 1.0)
    scales = [scale * inverse for scale in scales]
    blended = []
    for h in range(heads):
        part = slice(h * size, (h + 1) * size)
        blended.append(
            sum(
                ref[part].astype(f32) * scale[h : h + 1]
                for ref, scale in zip(part_refs, scales)
            )
        )
    value = jnp.concatenate(blended, axis=0).T + bias_ref[...]
    out_ref[...] = jnp.where(value > 0, value, jnp.exp(value) - 1.0).astype(bf16)


def pairs(count, k):
    return [(i, i ^ k) for i in range(count)]


def body(
    n_row,
    n_col,
    source_features,
    target_features,
    weight,
    score_source,
    score_target,
    out_bias,
    block_list,
    block_count,
    edge_bits,
):
    heads, size = score_source.shape
    width = weight.shape[1]
    own_src = source_features.shape[1]
    own_dst = target_features.shape[0]
    src_blocks = own_src * n_row // BLK
    dst_blocks = own_dst * n_col // BLK
    split = (
        own_src % BLK == 0
        and own_dst % BLK == 0
        and n_row & (n_row - 1) == 0
        and n_col & (n_col - 1) == 0
    )
    vmem = pl.BlockSpec(memory_space=pltpu.VMEM)
    smem = pl.BlockSpec(memory_space=pltpu.SMEM)

    dst_own = pl.pallas_call(
        target_kernel,
        out_shape=jax.ShapeDtypeStruct((heads, own_dst), f32),
        in_specs=[vmem] * 3,
        out_specs=vmem,
    )(target_features, weight, score_target)

    if split:
        x = source_features
        even = [x] + [lax.ppermute(x, "row", pairs(n_row, k)) for k in range(2, n_row, 2)]
        odd = [lax.ppermute(y, "row", pairs(n_row, 1)) for y in even] if n_row > 1 else []
        xs = [y for both in zip(even, odd) for y in both] if odd else even
        ds = [dst_own] + [lax.ppermute(dst_own, "col", pairs(n_col, k)) for k in range(1, n_col)]
    else:
        xs = [lax.all_gather(source_features[0], "row", axis=0, tiled=True)]
        ds = [lax.all_gather(dst_own, "col", axis=1, tiled=True)]

    extra = 4 * heads
    if split:
        outs = [jax.ShapeDtypeStruct((width + extra, own_dst), bf16)] * n_col
    else:
        outs = [jax.ShapeDtypeStruct((width + extra, own_dst * n_col), bf16)]
    cfg = (heads, size, src_blocks, dst_blocks, len(xs), len(ds), "row", "col", split)
    chunks = pl.pallas_call(
        functools.partial(tile_kernel, cfg),
        out_shape=outs,
        in_specs=[smem, smem] + [vmem] * (3 + len(xs) + len(ds)),
        out_specs=[vmem] * len(outs),
        scratch_shapes=[
            pltpu.VMEM((src_blocks, width, BLK), bf16),
            pltpu.VMEM((src_blocks * heads, BLK, BLK), f32),
            pltpu.VMEM((dst_blocks, heads, BLK), f32),
            pltpu.VMEM((dst_blocks * heads, 8, BLK), f32),
            pltpu.VMEM((dst_blocks * heads, 8, BLK), f32),
            pltpu.VMEM((dst_blocks, width, BLK), f32),
        ],
    )(block_list, block_count, edge_bits, weight, score_source, *xs, *ds)

    if not split:
        me = lax.axis_index("col")
        chunks = [
            lax.dynamic_slice_in_dim(chunks[0], (me ^ k) * own_dst, own_dst, 1)
            for k in range(n_col)
        ]
    parts = [chunks[0]] + [
        lax.ppermute(chunks[k], "col", pairs(n_col, k)) for k in range(1, n_col)
    ]
    return pl.pallas_call(
        functools.partial(merge_kernel, heads),
        out_shape=jax.ShapeDtypeStruct((own_dst, width), bf16),
        in_specs=[vmem] * (len(parts) + 1),
        out_specs=vmem,
    )(*parts, out_bias.reshape(1, width))


def solution(mesh):
    placed = (
        P("col", "row", None),
        P(("row", "col"), None),
        P(),
        P(),
        P(),
        P(),
        P("row", "col", None),
        P("row", "col"),
        P("row", "col", None, None, None),
    )
    return jax.shard_map(
        functools.partial(body, mesh.shape["row"], mesh.shape["col"]),
        mesh=mesh,
        in_specs=placed,
        out_specs=P(("row", "col"), None),
        check_vma=False,
    )
```
